32 devices in a mesh: gx: 4 (over z), gy: 8 (over y, x, core).
Axes of the slice: x: 2, y: 2, z: 4, core: 2. Of those that a mesh axis runs over, the one named last changes fastest.
Arguments:
- right_side: float32 [16384, 128], P(('gx', 'gy')), may hold values from -6 to 6
- prec_diag: float32 [16384], P(('gx', 'gy')), may hold values from 3 to 6
- prec_values: float32 [8, 16384], P(None, ('gx', 'gy')), may hold values from -0.6 to 0.2
- prec_columns: int32 [8, 16384], P(None, ('gx', 'gy')), may hold values from 0 to 1023
- inverse: bfloat16 [32, 1024, 1024], P(('gx', 'gy')), may hold values from -1 to 1
- send_list: int32 [32, 4, 128], P(('gx', 'gy')), may hold values from 0 to 511, as said below
- send_count: int32 [32, 4], P(('gx', 'gy')), may hold values from 32 to 128, as said below
- own_weight: float32 [16384], P(('gx', 'gy')), may hold values from 0.2 to 5
- copy_weight: float32 [32, 4, 128], P(('gx', 'gy')), may hold values from 0.2 to 5
Outputs:
- solution: float32 [16384, 128], P(('gx', 'gy'))
- residual: float32 [16384, 128], P(('gx', 'gy'))
The draws below stay inside these ranges and needn't reach their ends.
Inputs may be any that keep to these rules, and one draw needn't show every extreme that they name: `send_list`: the 128 entries of one subdomain and direction are distinct owned nodes. `send_count`: every subdomain has 128 live entries in at least one direction.
All inputs are finite; a program needn't handle non-finite values.
Results may differ from the reference program's by a relative error of at most 0.0072.
Values may be sent and summed in bfloat16 or wider, within the bound.
A program may use at most 64 MiB of HBM per device.

```python
import math
import jax
import jax.numpy as jnp
from jax import lax

SUB = 1024
SEND = 128
NNZ = 8
RHS = 128
ITERS = 2
OWN = 512
NODES = 16384
N_GX = 4
N_GY = 8
DEVICES = 32


def draw_send_list(key, part):
    keys_all = jax.random.split(key, DEVICES * 4)
    orders = jax.vmap(lambda single: jax.random.permutation(single, OWN)[:SEND])(keys_all)
    return orders.reshape(DEVICES, 4, SEND).astype(jnp.int32)


def draw_send_count(key, part):
    key_first, key_second = jax.random.split(key)
    counts = jax.random.randint(key_first, (DEVICES, 4), SEND // 4, SEND + 1)
    fullest = jax.random.randint(key_second, (DEVICES, 1), 0, 4)
    sides = jnp.arange(4, dtype=jnp.int32)[None, :]
    return jnp.where(sides == fullest, SEND, counts).astype(jnp.int32)


def draw_inverse(key, part):
    key_diag, key_rest = jax.random.split(key)
    diagonal = jax.random.uniform(key_diag, (DEVICES, SUB), jnp.float32, 0.15, 0.35)
    coupling = jax.random.normal(key_rest, (DEVICES, SUB, SUB), jnp.float32) * (0.1 / math.sqrt(SUB))
    return (coupling + diagonal[:, :, None] * jnp.eye(SUB, dtype=jnp.float32)).astype(jnp.bfloat16)


def with_ends(values, rng, least, largest):
    longest = values.shape.index(max(values.shape))
    spots = []
    for shift in (0, 1):
        where = [jax.random.randint(jax.random.fold_in(rng, axis), (), 0, length) for axis, length in enumerate(values.shape)]
        where[longest] = (where[longest] + shift) % values.shape[longest]
        spots.append(tuple(where))
    return values.at[spots[0]].set(least).at[spots[1]].set(largest)


def shard_levels(rng, shape, cuts, low, largest):
    gain = 1.0
    for position, parts in cuts:
        steps = jax.random.uniform(jax.random.fold_in(jax.random.fold_in(rng, 6), position), (parts,), jnp.float32, low / len(cuts), largest / len(cuts))
        gain = gain * jnp.repeat(jnp.exp(steps), shape[position] // parts).reshape((-1,) + (1,) * (len(shape) - 1 - position))
    return gain


def normal_values(key, dims, deviation, reach, cuts=(), kind=jnp.bfloat16):
    factor_of = shard_levels(key, dims, cuts, -0.22, 0.18) if cuts else 1.0
    values = jax.random.normal(key, dims, jnp.float32) * deviation * factor_of
    return jnp.minimum(jnp.maximum(values, -reach), reach).astype(kind)


def setup_inputs(seed: int = 0) -> dict:
    key_list = jax.random.split(jax.random.key(seed), 10)
    right_side = normal_values(key_list[0], (NODES, RHS), 1.0, 6.0, ((0, 32),), jnp.float32)
    prec_diag = jnp.clip(3.0 + 3.0 * jax.random.uniform(key_list[1], (NODES,), jnp.float32) ** shard_levels(key_list[1], (NODES,), ((0, 32),), -0.2, 0.2), 3.0, 6.0)
    prec_values = jnp.clip(-0.6 + 0.8 * jax.random.uniform(key_list[2], (NNZ, NODES), jnp.float32) ** shard_levels(key_list[2], (NNZ, NODES), ((1, 32),), -0.2, 0.2), -0.6, 0.2)
    prec_columns = with_ends(jax.random.randint(key_list[3], (NNZ, NODES), 0, SUB), jax.random.fold_in(key_list[3], 1), 0, SUB - 1).astype(jnp.int32)
    inverse = draw_inverse(jax.random.fold_in(key_list[9], 71), 0)
    send_list = draw_send_list(jax.random.fold_in(key_list[9], 71), 0)
    send_count = draw_send_count(jax.random.fold_in(key_list[9], 71), 0)
    own_weight = jnp.clip(jnp.exp(math.log(5.0) - 3.218876 * jax.random.uniform(key_list[7], (NODES,), jnp.float32) ** shard_levels(key_list[7], (NODES,), ((0, 32),), -0.2, 0.2)), 0.2, 5.0)
    copy_weight = jnp.clip(jnp.exp(math.log(5.0) - 3.218876 * jax.random.uniform(key_list[8], (DEVICES, 4, SEND), jnp.float32) ** shard_levels(key_list[8], (DEVICES, 4, SEND), ((0, 32),), -0.2, 0.2)), 0.2, 5.0)
    return dict(right_side=right_side, prec_diag=prec_diag, prec_values=prec_values, prec_columns=prec_columns, inverse=inverse, send_list=send_list, send_count=send_count, own_weight=own_weight, copy_weight=copy_weight)


LOWER = 0.25
UPPER = 2.0


def shift_down(array, axis_at):
    zero_edge = jnp.zeros_like(lax.slice_in_dim(array, 0, 1, axis=axis_at))
    return jnp.concatenate([zero_edge, lax.slice_in_dim(array, 0, array.shape[axis_at] - 1, axis=axis_at)], axis=axis_at)


def shift_up(array, axis_at):
    zero_edge = jnp.zeros_like(lax.slice_in_dim(array, 0, 1, axis=axis_at))
    return jnp.concatenate([lax.slice_in_dim(array, 1, array.shape[axis_at], axis=axis_at), zero_edge], axis=axis_at)


def neighbour_blocks(blocks):
    moved = [shift_down(blocks[:, :, 1], 0), shift_up(blocks[:, :, 0], 0), shift_down(blocks[:, :, 3], 1), shift_up(blocks[:, :, 2], 1)]
    return jnp.stack(moved, axis=2).reshape(DEVICES, 4, SEND, RHS)


def side_live():
    row_place = jnp.arange(N_GX, dtype=jnp.int32)[:, None] + jnp.zeros((N_GX, N_GY), jnp.int32)
    col_place = jnp.arange(N_GY, dtype=jnp.int32)[None, :] + jnp.zeros((N_GX, N_GY), jnp.int32)
    flags_all = jnp.stack([row_place > 0, row_place < N_GX - 1, col_place > 0, col_place < N_GY - 1], axis=2)
    return flags_all.reshape(DEVICES, 4)


def pack_rows(vector, send_list, send_count):
    per_device = vector.reshape(DEVICES, OWN, RHS)
    slot_ids = jnp.arange(SEND, dtype=jnp.int32)
    filled = slot_ids[None, None, :] < send_count[:, :, None]
    picked = jax.vmap(lambda rows_of, chosen: rows_of[chosen])(per_device, send_list)
    return jnp.where(filled[..., None], picked, 0.0).reshape(N_GX, N_GY, 4, SEND, RHS)


def precision_apply(vector, ghosts, prec_diag, prec_values, prec_columns):
    own_rows = vector.reshape(DEVICES, OWN, RHS)
    extended = jnp.concatenate([own_rows, ghosts.reshape(DEVICES, 4 * SEND, RHS)], axis=1)
    columns = prec_columns.reshape(NNZ, DEVICES, OWN).transpose(1, 0, 2)
    values = prec_values.reshape(NNZ, DEVICES, OWN).transpose(1, 0, 2)

    def one_device(members):
        ext_rows, cols_here, vals_here = members
        return jnp.sum(vals_here[:, :, None] * ext_rows[cols_here], axis=0)

    coupled = lax.map(one_device, (extended, columns, values))
    return prec_diag[:, None] * vector + coupled.reshape(NODES, RHS)


def precondition(vector, inverse, send_list, send_count, own_weight, slot_weight):
    ghosts = neighbour_blocks(pack_rows(vector, send_list, send_count)).reshape(DEVICES, 4 * SEND, RHS)
    stacked = jnp.concatenate([vector.reshape(DEVICES, OWN, RHS), ghosts], axis=1).astype(jnp.bfloat16)

    def solve_one(members):
        matrix, operand = members
        return jnp.dot(matrix.astype(jnp.float32), operand.astype(jnp.float32), precision=lax.Precision.HIGHEST)

    result = lax.map(solve_one, (inverse, stacked))
    returned_all = neighbour_blocks(result[:, OWN:].reshape(N_GX, N_GY, 4, SEND, RHS))

    def combine(owned_part, returned, chosen, weights_here, own_here):
        numerator = own_here[:, None] * owned_part
        numerator = numerator.at[chosen.reshape(-1)].add((weights_here[:, :, None] * returned).reshape(-1, RHS))
        denominator = own_here.at[chosen.reshape(-1)].add(weights_here.reshape(-1))
        return numerator / denominator[:, None]

    merged = jax.vmap(combine)(result[:, :OWN], returned_all, send_list, slot_weight, own_weight.reshape(DEVICES, OWN))
    return merged.reshape(NODES, RHS)


def reference(right_side, prec_diag, prec_values, prec_columns, inverse, send_list, send_count, own_weight, copy_weight):
    slot_ids = jnp.arange(SEND, dtype=jnp.int32)
    inside = (slot_ids[None, None, :] < send_count[:, :, None]) & side_live()[:, :, None]
    slot_weight = jnp.where(inside, copy_weight, 0.0)
    center = 0.5 * (UPPER + LOWER)
    spread = 0.5 * (UPPER - LOWER)
    sigma_ratio = center / spread
    solution = jnp.zeros_like(right_side)
    residual = right_side
    direction = precondition(residual, inverse, send_list, send_count, own_weight, slot_weight) / center
    ratio_now = 1.0 / sigma_ratio
    for iteration in range(ITERS):
        solution = solution + direction
        ghosts = neighbour_blocks(pack_rows(direction, send_list, send_count))
        residual = residual - precision_apply(direction, ghosts, prec_diag, prec_values, prec_columns)
        if iteration < ITERS - 1:
            update = precondition(residual, inverse, send_list, send_count, own_weight, slot_weight)
            ratio_next = 1.0 / (2.0 * sigma_ratio - ratio_now)
            direction = ratio_next * ratio_now * direction + (2.0 * ratio_next / spread) * update
            ratio_now = ratio_next
    return solution, residual
```

```python
import functools

import jax
import jax.numpy as jnp
from jax import lax
from jax.experimental import pallas as pl
from jax.experimental.pallas import tpu as pltpu
from jax.sharding import PartitionSpec as P

ITERS = 2
LOWER = 0.25
UPPER = 2.0

MESH = pl.DeviceIdType.MESH
LANES = 128
F32 = jnp.float32
BF16 = jnp.bfloat16


def dot_nn(left, right):
    return lax.dot_general(left, right, (((1,), (0,)), ((), ())), preferred_element_type=F32)


def dot_nt(left, right):
    return lax.dot_general(left, right, (((1,), (1,)), ((), ())), preferred_element_type=F32)


def kernel(
    n_x,
    n_y,
    right_ref,
    diag_ref,
    values_ref,
    columns_ref,
    inverse_hbm,
    list_ref,
    count_ref,
    own_ref,
    copy_ref,
    solution_ref,
    residual_ref,
    inverse,
    pick,
    coupling,
    send,
    recv,
    inverse_sem,
    send_sem,
    recv_sem,
):
    row = lax.axis_index("gx")
    col = lax.axis_index("gy")
    live = (row > 0, row < n_x - 1, col > 0, col < n_y - 1)
    target = ((row - 1, col), (row + 1, col), (row, col - 1), (row, col + 1))
    own = right_ref.shape[0]
    slots = list_ref.shape[2]
    entries = values_ref.shape[0]
    total = inverse.shape[0]
    rounds = recv.shape[0]

    load = pltpu.make_async_copy(inverse_hbm.at[0], inverse, inverse_sem)
    load.start()

    barrier = pltpu.get_barrier_semaphore()
    for k in range(4):

        @pl.when(live[k])
        def _():
            pl.semaphore_signal(barrier, inc=1, device_id=target[k], device_id_type=MESH)

    residual = jnp.transpose(right_ref[...])

    slot_id = lax.broadcasted_iota(jnp.int32, (1, slots), 1)
    node_id = lax.broadcasted_iota(jnp.int32, (own, slots), 0)
    weights = []
    for k in range(4):
        filled = slot_id < count_ref[0, k]
        chosen = jnp.where(filled, list_ref[0, k : k + 1, :], -1)
        pick[:, k * slots : (k + 1) * slots] = jnp.where(node_id == chosen, 1.0, 0.0).astype(BF16)
        inside = slot_id < jnp.where(live[k], count_ref[0, k], 0)
        weights.append(jnp.where(inside, copy_ref[0, k : k + 1, :], 0.0))
    weight = jnp.concatenate(weights, axis=1)

    for k in range(4):

        @pl.when(jnp.logical_not(live[k]))
        def _():
            for stage in range(rounds):
                recv[stage, k] = jnp.zeros(recv.shape[2:], recv.dtype)

    def copy(stage, k, peer):
        return pltpu.make_async_remote_copy(
            src_ref=send.at[stage, k],
            dst_ref=recv.at[stage, peer],
            send_sem=send_sem.at[stage, k],
            recv_sem=recv_sem.at[stage, peer],
            device_id=target[k],
            device_id_type=MESH,
        )

    def start(stage, blocks):
        for k in range(4):
            send[stage, k] = blocks[:, k * slots : (k + 1) * slots].astype(BF16)
        for k in range(4):

            @pl.when(live[k])
            def _():
                copy(stage, k, k ^ 1).start()

    def finish(stage):
        for k in range(4):

            @pl.when(live[k])
            def _():
                copy(stage, k, k).wait_recv()

        return jnp.concatenate([recv[stage, k] for k in range(4)], axis=1)

    def build_coupling(first, last):
        step = 16
        base = lax.broadcasted_iota(jnp.int32, (step, LANES), 0)
        for tile in range(own // LANES):
            lanes = slice(tile * LANES, (tile + 1) * LANES)
            columns = [jnp.broadcast_to(columns_ref[j : j + 1, lanes], (step, LANES)) for j in range(entries)]
            values = [jnp.broadcast_to(values_ref[j : j + 1, lanes], (step, LANES)) for j in range(entries)]

            def body(m, carry):
                here = base + m * step
                parts = [jnp.where(columns[j] == here, values[j], 0.0) for j in range(entries)]
                while len(parts) > 1:
                    parts = [sum(parts[i : i + 2][1:], parts[i]) for i in range(0, len(parts), 2)]
                coupling[pl.ds(pl.multiple_of(m * step, step), step), lanes] = parts[0].astype(BF16)
                return carry

            lax.fori_loop(first // step, last // step, body, 0, unroll=4)

    center = 0.5 * (UPPER + LOWER)
    spread = 0.5 * (UPPER - LOWER)
    sigma = center / spread
    diag = diag_ref[...]
    own_weight = own_ref[...]

    picked = dot_nn(residual.astype(BF16), pick[...])

    pl.semaphore_wait(barrier, sum(jnp.where(here, 1, 0) for here in live))

    ratio = 1.0 / sigma
    direction = None
    solution = None
    stage = 0
    inverse_denominator = None
    for iteration in range(ITERS):
        start(stage, picked)
        half = residual.astype(BF16)
        if iteration == 0:
            high = weight.astype(BF16)
            rest = weight - high.astype(F32)
            middle = rest.astype(BF16)
            low = (rest - middle.astype(F32)).astype(BF16)
            pieces = jnp.concatenate([jnp.broadcast_to(x, (16, 4 * slots)) for x in (high, middle, low)], axis=0)
            spread_weight = dot_nt(pieces, pick[...])
            denominator = own_weight + (spread_weight[0:1] + spread_weight[16:17] + spread_weight[32:33])
            inverse_denominator = 1.0 / denominator
            build_coupling(0, total // 2)
            load.wait()
        term_ghost = dot_nt(half, inverse[own:, :own])
        term_own = dot_nt(half, inverse[:own, :own])
        ghosts = finish(stage)
        start(stage + 1, term_ghost + dot_nt(ghosts, inverse[own:, own:]))
        term_own = term_own + dot_nt(ghosts, inverse[:own, own:])
        if iteration == 0:
            build_coupling(total // 2, total)
        returned = finish(stage + 1)
        weighted = (weight * returned.astype(F32)).astype(BF16)
        update = (own_weight * term_own + dot_nt(weighted, pick[...])) * inverse_denominator
        if iteration == 0:
            direction = update * (1.0 / center)
        else:
            ratio_next = 1.0 / (2.0 * sigma - ratio)
            direction = (ratio_next * ratio) * direction + (2.0 * ratio_next / spread) * update
            ratio = ratio_next
        half = direction.astype(BF16)
        start(stage + 2, dot_nn(half, pick[...]))
        solution = direction if solution is None else solution + direction
        residual = residual - diag * direction - dot_nn(half, coupling[:own, :])
        if iteration == ITERS - 1:
            solution_ref[...] = jnp.transpose(solution)
        ghosts = finish(stage + 2)
        residual = residual - dot_nn(ghosts, coupling[own:, :])
        if iteration < ITERS - 1:
            picked = dot_nn(residual.astype(BF16), pick[...])
        stage += 3
    residual_ref[...] = jnp.transpose(residual)

    for stage in range(rounds):
        for k in range(4):

            @pl.when(live[k])
            def _():
                copy(stage, k, k ^ 1).wait_send()


def per_device(n_x, n_y, right_side, prec_diag, prec_values, prec_columns, inverse, send_list, send_count, own_weight, copy_weight):
    own, width = right_side.shape
    total = inverse.shape[1]
    slots = send_list.shape[2]
    rounds = 3 * ITERS
    vmem = pl.BlockSpec(memory_space=pltpu.VMEM)
    out = jax.ShapeDtypeStruct((own, width), F32)
    return pl.pallas_call(
        functools.partial(kernel, n_x, n_y),
        out_shape=(out, out),
        in_specs=[
            vmem,
            vmem,
            vmem,
            vmem,
            pl.BlockSpec(memory_space=pl.ANY),
            vmem,
            pl.BlockSpec(memory_space=pltpu.SMEM),
            vmem,
            vmem,
        ],
        out_specs=(vmem, vmem),
        scratch_shapes=[
            pltpu.VMEM((total, total), BF16),
            pltpu.VMEM((own, 4 * slots), BF16),
            pltpu.VMEM((total, own), BF16),
            pltpu.VMEM((rounds, 4, width, slots), BF16),
            pltpu.VMEM((rounds, 4, width, slots), BF16),
            pltpu.SemaphoreType.DMA,
            pltpu.SemaphoreType.DMA((rounds, 4)),
            pltpu.SemaphoreType.DMA((rounds, 4)),
        ],
        compiler_params=pltpu.CompilerParams(collective_id=0, has_side_effects=True),
    )(
        right_side,
        prec_diag.reshape(1, own),
        prec_values,
        prec_columns,
        inverse,
        send_list,
        send_count,
        own_weight.reshape(1, own),
        copy_weight,
    )


def solution(mesh):
    return jax.shard_map(
        functools.partial(per_device, mesh.shape["gx"], mesh.shape["gy"]),
        mesh=mesh,
        in_specs=(
            P(("gx", "gy"), None),
            P(("gx", "gy")),
            P(None, ("gx", "gy")),
            P(None, ("gx", "gy")),
            P(("gx", "gy"), None, None),
            P(("gx", "gy"), None, None),
            P(("gx", "gy"), None),
            P(("gx", "gy")),
            P(("gx", "gy"), None, None),
        ),
        out_specs=(P(("gx", "gy"), None), P(("gx", "gy"), None)),
        check_vma=False,
    )
```

```python
import functools

import jax
import jax.numpy as jnp
from jax import lax
from jax.experimental import pallas as pl
from jax.experimental.pallas import tpu as pltpu
from jax.sharding import PartitionSpec as P

ITERS = 2
LOWER = 0.25
UPPER = 2.0

MESH = pl.DeviceIdType.MESH
LANES = 128
F32 = jnp.float32
BF16 = jnp.bfloat16


def dot_nn(left, right):
    return lax.dot_general(left, right, (((1,), (0,)), ((), ())), preferred_element_type=F32)


def dot_nt(left, right):
    return lax.dot_general(left, right, (((1,), (1,)), ((), ())), preferred_element_type=F32)


def kernel(
    n_x,
    n_y,
    right_hbm,
    diag_hbm,
    values_hbm,
    columns_hbm,
    inverse_hbm,
    list_hbm,
    count_ref,
    own_hbm,
    copy_hbm,
    solution_ref,
    residual_ref,
    right_ref,
    diag_ref,
    values_ref,
    columns_ref,
    list_ref,
    own_ref,
    copy_ref,
    inverse,
    pick,
    coupling,
    send,
    recv,
    load_sem,
    send_sem,
    recv_sem,
):
    row = lax.axis_index("gx")
    col = lax.axis_index("gy")
    live = (row > 0, row < n_x - 1, col > 0, col < n_y - 1)
    target = ((row - 1, col), (row + 1, col), (row, col - 1), (row, col + 1))
    own = right_ref.shape[0]
    slots = list_ref.shape[1]
    entries = values_ref.shape[0]
    total = inverse.shape[0]
    rounds = recv.shape[0]

    barrier = pltpu.get_barrier_semaphore()
    for k in range(4):

        @pl.when(live[k])
        def _():
            pl.semaphore_signal(barrier, inc=1, device_id=target[k], device_id_type=MESH)

    loads = [
        pltpu.make_async_copy(source, place, load_sem.at[i])
        for i, (source, place) in enumerate(
            (
                (list_hbm.at[0], list_ref),
                (right_hbm, right_ref),
                (copy_hbm.at[0], copy_ref),
                (columns_hbm, columns_ref),
                (values_hbm, values_ref),
                (own_hbm, own_ref),
                (diag_hbm, diag_ref),
                (inverse_hbm.at[0], inverse),
            )
        )
    ]
    for load in loads:
        load.start()
    loads[0].wait()
    slot_id = lax.broadcasted_iota(jnp.int32, (1, slots), 1)
    node_id = lax.broadcasted_iota(jnp.int32, (own, slots), 0)
    for k in range(4):
        filled = slot_id < count_ref[0, k]
        chosen = jnp.where(filled, list_ref[k : k + 1, :], -1)
        pick[:, k * slots : (k + 1) * slots] = jnp.where(node_id == chosen, 1.0, 0.0).astype(BF16)

    loads[1].wait()
    residual = jnp.transpose(right_ref[...])

    for k in range(4):

        @pl.when(jnp.logical_not(live[k]))
        def _():
            for stage in range(rounds):
                recv[stage, k] = jnp.zeros(recv.shape[2:], recv.dtype)

    def copy(stage, k, peer):
        return pltpu.make_async_remote_copy(
            src_ref=send.at[stage, k],
            dst_ref=recv.at[stage, peer],
            send_sem=send_sem.at[stage, k],
            recv_sem=recv_sem.at[stage, peer],
            device_id=target[k],
            device_id_type=MESH,
        )

    def start(stage, blocks):
        for k in range(4):
            send[stage, k] = blocks[:, k * slots : (k + 1) * slots].astype(BF16)
        for k in range(4):

            @pl.when(live[k])
            def _():
                copy(stage, k, k ^ 1).start()

    def finish(stage):
        for k in range(4):

            @pl.when(live[k])
            def _():
                copy(stage, k, k).wait_recv()

        return jnp.concatenate([recv[stage, k] for k in range(4)], axis=1)

    def build_coupling(first, last):
        step = 16
        base = lax.broadcasted_iota(jnp.int32, (step, LANES), 0)
        for tile in range(own // LANES):
            lanes = slice(tile * LANES, (tile + 1) * LANES)
            columns = [jnp.broadcast_to(columns_ref[j : j + 1, lanes], (step, LANES)) for j in range(entries)]
            values = [jnp.broadcast_to(values_ref[j : j + 1, lanes], (step, LANES)) for j in range(entries)]

            def body(m, carry):
                here = base + m * step
                parts = [jnp.where(columns[j] == here, values[j], 0.0) for j in range(entries)]
                while len(parts) > 1:
                    parts = [sum(parts[i : i + 2][1:], parts[i]) for i in range(0, len(parts), 2)]
                coupling[pl.ds(pl.multiple_of(m * step, step), step), lanes] = parts[0].astype(BF16)
                return carry

            lax.fori_loop(first // step, last // step, body, 0, unroll=4)

    center = 0.5 * (UPPER + LOWER)
    spread = 0.5 * (UPPER - LOWER)
    sigma = center / spread
    picked = dot_nn(residual.astype(BF16), pick[...])

    pl.semaphore_wait(barrier, sum(jnp.where(here, 1, 0) for here in live))

    ratio = 1.0 / sigma
    direction = None
    solution = None
    stage = 0
    inverse_denominator = None
    for iteration in range(ITERS):
        start(stage, picked)
        half = residual.astype(BF16)
        if iteration == 0:
            for load in loads[2:7]:
                load.wait()
            diag = diag_ref[...]
            own_weight = own_ref[...]
            weights = []
            for k in range(4):
                inside = slot_id < jnp.where(live[k], count_ref[0, k], 0)
                weights.append(jnp.where(inside, copy_ref[k : k + 1, :], 0.0))
            weight = jnp.concatenate(weights, axis=1)
            high = weight.astype(BF16)
            rest = weight - high.astype(F32)
            middle = rest.astype(BF16)
            low = (rest - middle.astype(F32)).astype(BF16)
            pieces = jnp.concatenate([jnp.broadcast_to(x, (16, 4 * slots)) for x in (high, middle, low)], axis=0)
            spread_weight = dot_nt(pieces, pick[...])
            denominator = own_weight + (spread_weight[0:1] + spread_weight[16:17] + spread_weight[32:33])
            inverse_denominator = 1.0 / denominator
            build_coupling(0, total // 2)
            loads[7].wait()
        term_ghost = dot_nt(half, inverse[own:, :own])
        term_own = dot_nt(half, inverse[:own, :own])
        ghosts = finish(stage)
        start(stage + 1, term_ghost + dot_nt(ghosts, inverse[own:, own:]))
        term_own = term_own + dot_nt(ghosts, inverse[:own, own:])
        if iteration == 0:
            build_coupling(total // 2, total)
        returned = finish(stage + 1)
        weighted = (weight * returned.astype(F32)).astype(BF16)
        update = (own_weight * term_own + dot_nt(weighted, pick[...])) * inverse_denominator
        if iteration == 0:
            direction = update * (1.0 / center)
        else:
            ratio_next = 1.0 / (2.0 * sigma - ratio)
            direction = (ratio_next * ratio) * direction + (2.0 * ratio_next / spread) * update
            ratio = ratio_next
        half = direction.astype(BF16)
        start(stage + 2, dot_nn(half, pick[...]))
        solution = direction if solution is None else solution + direction
        residual = residual - diag * direction - dot_nn(half, coupling[:own, :])
        if iteration == ITERS - 1:
            solution_ref[...] = solution
        ghosts = finish(stage + 2)
        residual = residual - dot_nn(ghosts, coupling[own:, :])
        if iteration < ITERS - 1:
            picked = dot_nn(residual.astype(BF16), pick[...])
        stage += 3
    residual_ref[...] = residual

    for stage in range(rounds):
        for k in range(4):

            @pl.when(live[k])
            def _():
                copy(stage, k, k ^ 1).wait_send()


def flip(solution_in, residual_in, solution_ref, residual_ref):
    solution_ref[...] = jnp.transpose(solution_in[...])
    residual_ref[...] = jnp.transpose(residual_in[...])


def per_device(n_x, n_y, right_side, prec_diag, prec_values, prec_columns, inverse, send_list, send_count, own_weight, copy_weight):
    own, width = right_side.shape
    total = inverse.shape[1]
    slots = send_list.shape[2]
    rounds = 3 * ITERS
    vmem = pl.BlockSpec(memory_space=pltpu.VMEM)
    hbm = pl.BlockSpec(memory_space=pltpu.HBM)
    field = pltpu.VMEM((width, own), F32)
    out = jax.ShapeDtypeStruct((own, width), F32)
    flipped = pl.pallas_call(
        functools.partial(kernel, n_x, n_y),
        out_shape=(field, field),
        in_specs=[hbm] * 6 + [pl.BlockSpec(memory_space=pltpu.SMEM)] + [hbm] * 2,
        out_specs=(vmem, vmem),
        scratch_shapes=[
            pltpu.VMEM(right_side.shape, F32),
            pltpu.VMEM((1, own), F32),
            pltpu.VMEM(prec_values.shape, F32),
            pltpu.VMEM(prec_columns.shape, jnp.int32),
            pltpu.VMEM((4, slots), jnp.int32),
            pltpu.VMEM((1, own), F32),
            pltpu.VMEM((4, slots), F32),
            pltpu.VMEM((total, total), BF16),
            pltpu.VMEM((own, 4 * slots), BF16),
            pltpu.VMEM((total, own), BF16),
            pltpu.VMEM((rounds, 4, width, slots), BF16),
            pltpu.VMEM((rounds, 4, width, slots), BF16),
            pltpu.SemaphoreType.DMA((8,)),
            pltpu.SemaphoreType.DMA((rounds, 4)),
            pltpu.SemaphoreType.DMA((rounds, 4)),
        ],
        compiler_params=pltpu.CompilerParams(collective_id=0, has_side_effects=True, vmem_limit_bytes=62 * 2**20 + 2**19),
    )(
        right_side,
        prec_diag.reshape(1, own),
        prec_values,
        prec_columns,
        inverse,
        send_list,
        send_count,
        own_weight.reshape(1, own),
        copy_weight,
    )
    return pl.pallas_call(
        flip,
        out_shape=(out, out),
        in_specs=[vmem, vmem],
        out_specs=(vmem, vmem),
        compiler_params=pltpu.CompilerParams(vmem_limit_bytes=16 * 2**20),
    )(*flipped)


def solution(mesh):
    return jax.shard_map(
        functools.partial(per_device, mesh.shape["gx"], mesh.shape["gy"]),
        mesh=mesh,
        in_specs=(
            P(("gx", "gy"), None),
            P(("gx", "gy")),
            P(None, ("gx", "gy")),
            P(None, ("gx", "gy")),
            P(("gx", "gy"), None, None),
            P(("gx", "gy"), None, None),
            P(("gx", "gy"), None),
            P(("gx", "gy")),
            P(("gx", "gy"), None, None),
        ),
        out_specs=(P(("gx", "gy"), None), P(("gx", "gy"), None)),
        check_vma=False,
    )
```

```python
import functools

import jax
import jax.numpy as jnp
from jax import lax
from jax.experimental import pallas as pl
from jax.experimental.pallas import tpu as pltpu
from jax.sharding import PartitionSpec as P

ITERS = 2
LOWER = 0.25
UPPER = 2.0

MESH = pl.DeviceIdType.MESH
LANES = 128
F32 = jnp.float32
BF16 = jnp.bfloat16
PARTS = 2
ORDER = (0, 1, 2, 3)


def dot_nn(left, right):
    return lax.dot_general(left, right, (((1,), (0,)), ((), ())), preferred_element_type=F32)


def dot_nt(left, right):
    return lax.dot_general(left, right, (((1,), (1,)), ((), ())), preferred_element_type=F32)


def kernel(
    n_x,
    n_y,
    right_hbm,
    diag_hbm,
    values_hbm,
    columns_hbm,
    inverse_hbm,
    list_hbm,
    count_ref,
    own_hbm,
    copy_hbm,
    solution_ref,
    residual_ref,
    right_ref,
    diag_ref,
    values_ref,
    columns_ref,
    list_ref,
    own_ref,
    copy_ref,
    inverse,
    pick,
    coupling,
    send,
    recv,
    load_sem,
    send_sem,
    recv_sem,
):
    row = lax.axis_index("gx")
    col = lax.axis_index("gy")
    live = (row > 0, row < n_x - 1, col > 0, col < n_y - 1)
    target = ((row - 1, col), (row + 1, col), (row, col - 1), (row, col + 1))
    own = right_ref.shape[0]
    slots = list_ref.shape[1]
    entries = values_ref.shape[0]
    total = inverse.shape[0]
    rounds = recv.shape[0]

    barrier = pltpu.get_barrier_semaphore()
    for k in range(4):

        @pl.when(live[k])
        def _():
            pl.semaphore_signal(barrier, inc=1, device_id=target[k], device_id_type=MESH)

    loads = [
        pltpu.make_async_copy(source, place, load_sem.at[i])
        for i, (source, place) in enumerate(
            (
                (list_hbm.at[0], list_ref),
                (right_hbm, right_ref),
                (copy_hbm.at[0], copy_ref),
                (columns_hbm, columns_ref),
                (values_hbm, values_ref),
                (own_hbm, own_ref),
                (diag_hbm, diag_ref),
                (inverse_hbm.at[0], inverse),
            )
        )
    ]
    for load in loads:
        load.start()
    loads[0].wait()
    slot_id = lax.broadcasted_iota(jnp.int32, (1, slots), 1)
    node_id = lax.broadcasted_iota(jnp.int32, (own, slots), 0)
    for k in range(4):
        filled = slot_id < count_ref[0, k]
        chosen = jnp.where(filled, list_ref[k : k + 1, :], -1)
        pick[:, k * slots : (k + 1) * slots] = jnp.where(node_id == chosen, 1.0, 0.0).astype(BF16)

    loads[1].wait()
    field = jnp.transpose(right_ref[...])
    rows = field.shape[0] // PARTS
    parts = range(PARTS)
    residual = [field[part * rows : (part + 1) * rows] for part in parts]

    for k in range(4):

        @pl.when(jnp.logical_not(live[k]))
        def _():
            for stage in range(rounds):
                for part in range(PARTS):
                    recv[stage, part, k] = jnp.zeros(recv.shape[3:], recv.dtype)

    def copy(stage, part, k, peer):
        turn = stage % 2
        return pltpu.make_async_remote_copy(
            src_ref=send.at[stage, part, k],
            dst_ref=recv.at[stage, part, peer],
            send_sem=send_sem.at[turn, part, k],
            recv_sem=recv_sem.at[turn, part, peer],
            device_id=target[k],
            device_id_type=MESH,
        )

    def start(stage, part, block):
        for k in ORDER:
            send[stage, part, k] = block(slice(k * slots, (k + 1) * slots)).astype(BF16)
        for k in ORDER:
            launch(stage, part, k)

    def launch(stage, part, k):
        @pl.when(live[k])
        def _():
            if stage >= 2:
                copy(stage - 2, part, k, k ^ 1).wait_send()
            copy(stage, part, k, k ^ 1).start()

    def finish(stage, part):
        for k in range(4):

            @pl.when(live[k])
            def _():
                copy(stage, part, k, k).wait_recv()

        return jnp.concatenate([recv[stage, part, k] for k in range(4)], axis=1)

    def build_coupling(first, last):
        step = 16
        base = lax.broadcasted_iota(jnp.int32, (step, LANES), 0)
        for tile in range(own // LANES):
            lanes = slice(tile * LANES, (tile + 1) * LANES)
            columns = [jnp.broadcast_to(columns_ref[j : j + 1, lanes], (step, LANES)) for j in range(entries)]
            values = [jnp.broadcast_to(values_ref[j : j + 1, lanes], (step, LANES)) for j in range(entries)]

            def body(m, carry):
                here = base + m * step
                parts = [jnp.where(columns[j] == here, values[j], 0.0) for j in range(entries)]
                while len(parts) > 1:
                    parts = [sum(parts[i : i + 2][1:], parts[i]) for i in range(0, len(parts), 2)]
                coupling[pl.ds(pl.multiple_of(m * step, step), step), lanes] = parts[0].astype(BF16)
                return carry

            lax.fori_loop(first // step, last // step, body, 0, unroll=4)

    center = 0.5 * (UPPER + LOWER)
    spread = 0.5 * (UPPER - LOWER)
    sigma = center / spread
    half = [x.astype(BF16) for x in residual]
    picked = [dot_nn(x, pick[...]).astype(BF16) for x in half]

    pl.semaphore_wait(barrier, sum(jnp.where(here, 1, 0) for here in live))

    for part in parts:
        start(0, part, lambda lanes: picked[part][:, lanes])

    ratio = 1.0 / sigma
    direction = [None] * PARTS
    solution = [None] * PARTS
    stage = 0
    for iteration in range(ITERS):
        if iteration == 0:
            for load in loads[2:7]:
                load.wait()
            diag = diag_ref[...]
            own_weight = own_ref[...]
            weights = []
            for k in range(4):
                inside = slot_id < jnp.where(live[k], count_ref[0, k], 0)
                weights.append(jnp.where(inside, copy_ref[k : k + 1, :], 0.0))
            weight = jnp.concatenate(weights, axis=1)
            high = weight.astype(BF16)
            rest = weight - high.astype(F32)
            middle = rest.astype(BF16)
            low = (rest - middle.astype(F32)).astype(BF16)
            pieces = jnp.concatenate([jnp.broadcast_to(x, (16, 4 * slots)) for x in (high, middle, low)], axis=0)
            spread_weight = dot_nt(pieces, pick[...])
            denominator = own_weight + (spread_weight[0:1] + spread_weight[16:17] + spread_weight[32:33])
            inverse_denominator = 1.0 / denominator
            build_coupling(0, total // 2)
            loads[7].wait()
        term_ghost = [dot_nt(x, inverse[own:, :own]) for x in half]
        term_own = [dot_nt(x, inverse[:own, :own]) for x in half]
        ghosts = [None] * PARTS
        for part in parts:
            ghosts[part] = finish(stage, part)
            whole = term_ghost[part] + dot_nt(ghosts[part], inverse[own:, own:])
            start(stage + 1, part, lambda lanes: whole[:, lanes])
        term_own = [own_weight * (term_own[part] + dot_nt(ghosts[part], inverse[:own, own:])) for part in parts]
        if iteration == 0:
            build_coupling(total // 2, total)
        else:
            ratio_next = 1.0 / (2.0 * sigma - ratio)
        for part in parts:
            returned = finish(stage + 1, part)
            weighted = (weight * returned.astype(F32)).astype(BF16)
            update = (term_own[part] + dot_nt(weighted, pick[...])) * inverse_denominator
            if iteration == 0:
                direction[part] = update * (1.0 / center)
            else:
                direction[part] = (ratio_next * ratio) * direction[part] + (2.0 * ratio_next / spread) * update
            half[part] = direction[part].astype(BF16)
            whole = dot_nn(half[part], pick[...])
            start(stage + 2, part, lambda lanes: whole[:, lanes])
        if iteration > 0:
            ratio = ratio_next
        for part in parts:
            solution[part] = direction[part] if iteration == 0 else solution[part] + direction[part]
            residual[part] = residual[part] - diag * direction[part] - dot_nn(half[part], coupling[:own, :])
            if iteration == ITERS - 1:
                solution_ref[part * rows : (part + 1) * rows, :] = solution[part]
        for part in parts:
            ghosts[part] = finish(stage + 2, part)
            residual[part] = residual[part] - dot_nn(ghosts[part], coupling[own:, :])
            if iteration < ITERS - 1:
                half[part] = residual[part].astype(BF16)
                whole = dot_nn(half[part], pick[...])
                start(stage + 3, part, lambda lanes: whole[:, lanes])
            else:
                residual_ref[part * rows : (part + 1) * rows, :] = residual[part]
        stage += 3

    for stage in range(max(rounds - 2, 0), rounds):
        for part in parts:
            for k in range(4):

                @pl.when(live[k])
                def _():
                    copy(stage, part, k, k ^ 1).wait_send()


def flip(solution_in, residual_in, solution_ref, residual_ref):
    solution_ref[...] = jnp.transpose(solution_in[...])
    residual_ref[...] = jnp.transpose(residual_in[...])


def per_device(n_x, n_y, right_side, prec_diag, prec_values, prec_columns, inverse, send_list, send_count, own_weight, copy_weight):
    own, width = right_side.shape
    total = inverse.shape[1]
    slots = send_list.shape[2]
    rounds = 3 * ITERS
    vmem = pl.BlockSpec(memory_space=pltpu.VMEM)
    hbm = pl.BlockSpec(memory_space=pltpu.HBM)
    field = pltpu.VMEM((width, own), F32)
    out = jax.ShapeDtypeStruct((own, width), F32)
    flipped = pl.pallas_call(
        functools.partial(kernel, n_x, n_y),
        out_shape=(field, field),
        in_specs=[hbm] * 6 + [pl.BlockSpec(memory_space=pltpu.SMEM)] + [hbm] * 2,
        out_specs=(vmem, vmem),
        scratch_shapes=[
            pltpu.VMEM(right_side.shape, F32),
            pltpu.VMEM((1, own), F32),
            pltpu.VMEM(prec_values.shape, F32),
            pltpu.VMEM(prec_columns.shape, jnp.int32),
            pltpu.VMEM((4, slots), jnp.int32),
            pltpu.VMEM((1, own), F32),
            pltpu.VMEM((4, slots), F32),
            pltpu.VMEM((total, total), BF16),
            pltpu.VMEM((own, 4 * slots), BF16),
            pltpu.VMEM((total, own), BF16),
            pltpu.VMEM((rounds, PARTS, 4, width // PARTS, slots), BF16),
            pltpu.VMEM((rounds, PARTS, 4, width // PARTS, slots), BF16),
            pltpu.SemaphoreType.DMA((8,)),
            pltpu.SemaphoreType.DMA((2, PARTS, 4)),
            pltpu.SemaphoreType.DMA((2, PARTS, 4)),
        ],
        compiler_params=pltpu.CompilerParams(collective_id=0, has_side_effects=True, vmem_limit_bytes=62 * 2**20 + 2**19),
    )(
        right_side,
        prec_diag.reshape(1, own),
        prec_values,
        prec_columns,
        inverse,
        send_list,
        send_count,
        own_weight.reshape(1, own),
        copy_weight,
    )
    return pl.pallas_call(
        flip,
        out_shape=(out, out),
        in_specs=[vmem, vmem],
        out_specs=(vmem, vmem),
        compiler_params=pltpu.CompilerParams(vmem_limit_bytes=16 * 2**20),
    )(*flipped)


def solution(mesh):
    return jax.shard_map(
        functools.partial(per_device, mesh.shape["gx"], mesh.shape["gy"]),
        mesh=mesh,
        in_specs=(
            P(("gx", "gy"), None),
            P(("gx", "gy")),
            P(None, ("gx", "gy")),
            P(None, ("gx", "gy")),
            P(("gx", "gy"), None, None),
            P(("gx", "gy"), None, None),
            P(("gx", "gy"), None),
            P(("gx", "gy")),
            P(("gx", "gy"), None, None),
        ),
        out_specs=(P(("gx", "gy"), None), P(("gx", "gy"), None)),
        check_vma=False,
    )
```

```python
import functools

import jax
import jax.numpy as jnp
from jax import lax
from jax.experimental import pallas as pl
from jax.experimental.pallas import tpu as pltpu
from jax.sharding import PartitionSpec as P

ITERS = 2
LOWER = 0.25
UPPER = 2.0

MESH = pl.DeviceIdType.MESH
LANES = 128
F32 = jnp.float32
BF16 = jnp.bfloat16
PARTS = 2
ORDER = (0, 1, 2, 3)


def dot_nn(left, right):
    return lax.dot_general(left, right, (((1,), (0,)), ((), ())), preferred_element_type=F32)


def dot_nt(left, right):
    return lax.dot_general(left, right, (((1,), (1,)), ((), ())), preferred_element_type=F32)


def kernel(
    n_x,
    n_y,
    right_hbm,
    diag_hbm,
    values_hbm,
    columns_hbm,
    inverse_hbm,
    list_hbm,
    count_ref,
    own_hbm,
    copy_hbm,
    solution_ref,
    residual_ref,
    right_ref,
    diag_ref,
    values_ref,
    columns_ref,
    list_ref,
    own_ref,
    copy_ref,
    inverse,
    pick,
    coupling,
    send,
    recv,
    ahead,
    held,
    load_sem,
    send_sem,
    recv_sem,
):
    row = lax.axis_index("gx")
    col = lax.axis_index("gy")
    live = (row > 0, row < n_x - 1, col > 0, col < n_y - 1)
    target = ((row - 1, col), (row + 1, col), (row, col - 1), (row, col + 1))
    own = right_ref.shape[0]
    slots = list_ref.shape[1]
    entries = values_ref.shape[0]
    total = inverse.shape[0]
    rounds = recv.shape[0]

    barrier = pltpu.get_barrier_semaphore()
    for k in range(4):

        @pl.when(live[k])
        def _():
            pl.semaphore_signal(barrier, inc=1, device_id=target[k], device_id_type=MESH)

    loads = [
        pltpu.make_async_copy(source, place, load_sem.at[i])
        for i, (source, place) in enumerate(
            (
                (list_hbm.at[0], list_ref),
                (right_hbm, right_ref),
                (copy_hbm.at[0], copy_ref),
                (columns_hbm, columns_ref),
                (values_hbm, values_ref),
                (own_hbm, own_ref),
                (diag_hbm, diag_ref),
                (inverse_hbm.at[0], inverse),
            )
        )
    ]
    for load in loads:
        load.start()
    loads[0].wait()
    slot_id = lax.broadcasted_iota(jnp.int32, (1, slots), 1)
    node_id = lax.broadcasted_iota(jnp.int32, (own, slots), 0)
    for k in range(4):
        filled = slot_id < count_ref[0, k]
        chosen = jnp.where(filled, list_ref[k : k + 1, :], -1)
        pick[:, k * slots : (k + 1) * slots] = jnp.where(node_id == chosen, 1.0, 0.0).astype(BF16)

    loads[1].wait()
    field = jnp.transpose(right_ref[...])
    rows = field.shape[0] // PARTS
    parts = range(PARTS)
    residual = [field[part * rows : (part + 1) * rows] for part in parts]

    for k in range(4):

        @pl.when(jnp.logical_not(live[k]))
        def _():
            for stage in range(rounds):
                for part in range(PARTS):
                    recv[stage, part, k] = jnp.zeros(recv.shape[3:], recv.dtype)

    def copy(stage, part, k, peer):
        turn = stage % 2
        return pltpu.make_async_remote_copy(
            src_ref=send.at[stage, part, k],
            dst_ref=recv.at[stage, part, peer],
            send_sem=send_sem.at[turn, part, k],
            recv_sem=recv_sem.at[turn, part, peer],
            device_id=target[k],
            device_id_type=MESH,
        )

    def start(stage, part, block):
        for k in ORDER:
            send[stage, part, k] = block(slice(k * slots, (k + 1) * slots)).astype(BF16)
        for k in ORDER:
            launch(stage, part, k)

    def launch(stage, part, k):
        @pl.when(live[k])
        def _():
            if stage >= 2:
                copy(stage - 2, part, k, k ^ 1).wait_send()
            copy(stage, part, k, k ^ 1).start()

    def finish(stage, part):
        for k in range(4):

            @pl.when(live[k])
            def _():
                copy(stage, part, k, k).wait_recv()

        return jnp.concatenate([recv[stage, part, k] for k in range(4)], axis=1)

    def build_coupling(first, last):
        step = 16
        base = lax.broadcasted_iota(jnp.int32, (step, LANES), 0)
        for tile in range(own // LANES):
            lanes = slice(tile * LANES, (tile + 1) * LANES)
            columns = [jnp.broadcast_to(columns_ref[j : j + 1, lanes], (step, LANES)) for j in range(entries)]
            values = [jnp.broadcast_to(values_ref[j : j + 1, lanes], (step, LANES)) for j in range(entries)]

            def body(m, carry):
                here = base + m * step
                parts = [jnp.where(columns[j] == here, values[j], 0.0) for j in range(entries)]
                while len(parts) > 1:
                    parts = [sum(parts[i : i + 2][1:], parts[i]) for i in range(0, len(parts), 2)]
                coupling[pl.ds(pl.multiple_of(m * step, step), step), lanes] = parts[0].astype(BF16)
                return carry

            lax.fori_loop(first // step, last // step, body, 0, unroll=4)

    center = 0.5 * (UPPER + LOWER)
    spread = 0.5 * (UPPER - LOWER)
    sigma = center / spread
    half = [x.astype(BF16) for x in residual]
    picked = [dot_nn(x, pick[...]).astype(BF16) for x in half]

    pl.semaphore_wait(barrier, sum(jnp.where(here, 1, 0) for here in live))

    for part in parts:
        start(0, part, lambda lanes: picked[part][:, lanes])

    ratio = 1.0 / sigma
    direction = [None] * PARTS
    solution = [None] * PARTS
    stage = 0
    for iteration in range(ITERS):
        if iteration == 0:
            for load in loads[2:7]:
                load.wait()
            diag = diag_ref[...]
            own_weight = own_ref[...]
            weights = []
            for k in range(4):
                inside = slot_id < jnp.where(live[k], count_ref[0, k], 0)
                weights.append(jnp.where(inside, copy_ref[k : k + 1, :], 0.0))
            weight = jnp.concatenate(weights, axis=1)
            high = weight.astype(BF16)
            rest = weight - high.astype(F32)
            middle = rest.astype(BF16)
            low = (rest - middle.astype(F32)).astype(BF16)
            pieces = jnp.concatenate([jnp.broadcast_to(x, (16, 4 * slots)) for x in (high, middle, low)], axis=0)
            spread_weight = dot_nt(pieces, pick[...])
            denominator = own_weight + (spread_weight[0:1] + spread_weight[16:17] + spread_weight[32:33])
            inverse_denominator = 1.0 / denominator
            build_coupling(0, total // 2)
            loads[7].wait()
        for part in parts:
            ahead[part] = dot_nt(half[part], inverse[own:, :own])
        for part in parts:
            held[part] = dot_nt(half[part], inverse[:own, :own])
        ghosts = [None] * PARTS
        for part in parts:
            ghosts[part] = finish(stage, part)
            whole = ahead[part] + dot_nt(ghosts[part], inverse[own:, own:])
            start(stage + 1, part, lambda lanes: whole[:, lanes])
        for part in parts:
            held[part] = own_weight * (held[part] + dot_nt(ghosts[part], inverse[:own, own:]))
        if iteration == 0:
            build_coupling(total // 2, total)
        else:
            ratio_next = 1.0 / (2.0 * sigma - ratio)
        for part in parts:
            returned = finish(stage + 1, part)
            weighted = (weight * returned.astype(F32)).astype(BF16)
            update = (held[part] + dot_nt(weighted, pick[...])) * inverse_denominator
            if iteration == 0:
                direction[part] = update * (1.0 / center)
            else:
                direction[part] = (ratio_next * ratio) * direction[part] + (2.0 * ratio_next / spread) * update
            half[part] = direction[part].astype(BF16)
            whole = dot_nn(half[part], pick[...])
            start(stage + 2, part, lambda lanes: whole[:, lanes])
        if iteration > 0:
            ratio = ratio_next
        for part in parts:
            solution[part] = direction[part] if iteration == 0 else solution[part] + direction[part]
            held[part] = residual[part] - diag * direction[part] - dot_nn(half[part], coupling[:own, :])
        if iteration == ITERS - 1:
            solution_ref[...] = jnp.transpose(jnp.concatenate(solution, axis=0))
        for part in parts:
            ghosts[part] = finish(stage + 2, part)
            residual[part] = held[part] - dot_nn(ghosts[part], coupling[own:, :])
            if iteration < ITERS - 1:
                half[part] = residual[part].astype(BF16)
                whole = dot_nn(half[part], pick[...])
                start(stage + 3, part, lambda lanes: whole[:, lanes])
            else:
                residual_ref[part * rows : (part + 1) * rows, :] = residual[part]
        stage += 3

    for stage in range(max(rounds - 2, 0), rounds):
        for part in parts:
            for k in range(4):

                @pl.when(live[k])
                def _():
                    copy(stage, part, k, k ^ 1).wait_send()


def write_out(solution_in, residual_in, solution_hbm, residual_hbm, flipped, sems):
    own = residual_in.shape[1]
    copies = [pltpu.make_async_copy(solution_in, solution_hbm, sems.at[0])]
    copies[0].start()
    for i in range(own // LANES):
        lanes = slice(i * LANES, (i + 1) * LANES)
        flipped[lanes, :] = jnp.transpose(residual_in[:, lanes])
        copies.append(pltpu.make_async_copy(flipped.at[lanes], residual_hbm.at[lanes], sems.at[1 + i]))
        copies[-1].start()
    for copy in copies:
        copy.wait()


def per_device(n_x, n_y, right_side, prec_diag, prec_values, prec_columns, inverse, send_list, send_count, own_weight, copy_weight):
    own, width = right_side.shape
    total = inverse.shape[1]
    slots = send_list.shape[2]
    rounds = 3 * ITERS
    vmem = pl.BlockSpec(memory_space=pltpu.VMEM)
    hbm = pl.BlockSpec(memory_space=pltpu.HBM)
    fields = (pltpu.VMEM((own, width), F32), pltpu.VMEM((width, own), F32))
    out = jax.ShapeDtypeStruct((own, width), F32)
    results = pl.pallas_call(
        functools.partial(kernel, n_x, n_y),
        out_shape=fields,
        in_specs=[hbm] * 6 + [pl.BlockSpec(memory_space=pltpu.SMEM)] + [hbm] * 2,
        out_specs=(vmem, vmem),
        scratch_shapes=[
            pltpu.VMEM(right_side.shape, F32),
            pltpu.VMEM((1, own), F32),
            pltpu.VMEM(prec_values.shape, F32),
            pltpu.VMEM(prec_columns.shape, jnp.int32),
            pltpu.VMEM((4, slots), jnp.int32),
            pltpu.VMEM((1, own), F32),
            pltpu.VMEM((4, slots), F32),
            pltpu.VMEM((total, total), BF16),
            pltpu.VMEM((own, 4 * slots), BF16),
            pltpu.VMEM((total, own), BF16),
            pltpu.VMEM((rounds, PARTS, 4, width // PARTS, slots), BF16),
            pltpu.VMEM((rounds, PARTS, 4, width // PARTS, slots), BF16),
            pltpu.VMEM((PARTS, width // PARTS, 4 * slots), F32),
            pltpu.VMEM((PARTS, width // PARTS, own), F32),
            pltpu.SemaphoreType.DMA((8,)),
            pltpu.SemaphoreType.DMA((2, PARTS, 4)),
            pltpu.SemaphoreType.DMA((2, PARTS, 4)),
        ],
        compiler_params=pltpu.CompilerParams(collective_id=0, has_side_effects=True, vmem_limit_bytes=62 * 2**20 + 2**19),
    )(
        right_side,
        prec_diag.reshape(1, own),
        prec_values,
        prec_columns,
        inverse,
        send_list,
        send_count,
        own_weight.reshape(1, own),
        copy_weight,
    )
    return pl.pallas_call(
        write_out,
        out_shape=(out, out),
        in_specs=[vmem, vmem],
        out_specs=(hbm, hbm),
        scratch_shapes=[pltpu.VMEM((own, width), F32), pltpu.SemaphoreType.DMA((1 + own // LANES,))],
        compiler_params=pltpu.CompilerParams(vmem_limit_bytes=16 * 2**20),
    )(*results)


def solution(mesh):
    return jax.shard_map(
        functools.partial(per_device, mesh.shape["gx"], mesh.shape["gy"]),
        mesh=mesh,
        in_specs=(
            P(("gx", "gy"), None),
            P(("gx", "gy")),
            P(None, ("gx", "gy")),
            P(None, ("gx", "gy")),
            P(("gx", "gy"), None, None),
            P(("gx", "gy"), None, None),
            P(("gx", "gy"), None),
            P(("gx", "gy")),
            P(("gx", "gy"), None, None),
        ),
        out_specs=(P(("gx", "gy"), None), P(("gx", "gy"), None)),
        check_vma=False,
    )
```

```python
import functools

import jax
import jax.numpy as jnp
from jax import lax
from jax.experimental import pallas as pl
from jax.experimental.pallas import tpu as pltpu
from jax.sharding import PartitionSpec as P

ITERS = 2
LOWER = 0.25
UPPER = 2.0

MESH = pl.DeviceIdType.MESH
LANES = 128
F32 = jnp.float32
BF16 = jnp.bfloat16
PARTS = 2
ORDER = (0, 1, 2, 3)


def dot_nn(left, right):
    return lax.dot_general(left, right, (((1,), (0,)), ((), ())), preferred_element_type=F32)


def dot_nt(left, right):
    return lax.dot_general(left, right, (((1,), (1,)), ((), ())), preferred_element_type=F32)


def kernel(
    n_x,
    n_y,
    right_hbm,
    diag_hbm,
    values_hbm,
    columns_hbm,
    inverse_hbm,
    list_hbm,
    count_hbm,
    own_hbm,
    copy_hbm,
    solution_ref,
    residual_ref,
    right_ref,
    diag_ref,
    values_ref,
    columns_ref,
    list_ref,
    count_ref,
    own_ref,
    copy_ref,
    inverse,
    pick,
    coupling,
    send,
    recv,
    ahead,
    held,
    load_sem,
    send_sem,
    recv_sem,
):
    row = lax.axis_index("gx")
    col = lax.axis_index("gy")
    live = (row > 0, row < n_x - 1, col > 0, col < n_y - 1)
    target = ((row - 1, col), (row + 1, col), (row, col - 1), (row, col + 1))
    own = right_ref.shape[0]
    slots = list_ref.shape[1]
    entries = values_ref.shape[0]
    total = inverse.shape[0]
    rounds = recv.shape[0]

    barrier = pltpu.get_barrier_semaphore()
    for k in range(4):

        @pl.when(live[k])
        def _():
            pl.semaphore_signal(barrier, inc=1, device_id=target[k], device_id_type=MESH)

    loads = [
        pltpu.make_async_copy(source, place, load_sem.at[i])
        for i, (source, place) in enumerate(
            (
                (count_hbm, count_ref),
                (list_hbm.at[0], list_ref),
                (right_hbm, right_ref),
                (copy_hbm.at[0], copy_ref),
                (columns_hbm, columns_ref),
                (values_hbm, values_ref),
                (own_hbm, own_ref),
                (diag_hbm, diag_ref),
                (inverse_hbm.at[0], inverse),
            )
        )
    ]
    for load in loads:
        load.start()
    loads[0].wait()
    loads[1].wait()
    slot_id = lax.broadcasted_iota(jnp.int32, (1, slots), 1)
    node_id = lax.broadcasted_iota(jnp.int32, (own, slots), 0)
    for k in range(4):
        filled = slot_id < count_ref[0, k]
        chosen = jnp.where(filled, list_ref[k : k + 1, :], -1)
        pick[:, k * slots : (k + 1) * slots] = jnp.where(node_id == chosen, 1.0, 0.0).astype(BF16)

    loads[2].wait()
    field = jnp.transpose(right_ref[...])
    rows = field.shape[0] // PARTS
    parts = range(PARTS)
    residual = [field[part * rows : (part + 1) * rows] for part in parts]

    for k in range(4):

        @pl.when(jnp.logical_not(live[k]))
        def _():
            for stage in range(rounds):
                for part in range(PARTS):
                    recv[stage, part, k] = jnp.zeros(recv.shape[3:], recv.dtype)

    def copy(stage, part, k, peer):
        turn = stage % 2
        return pltpu.make_async_remote_copy(
            src_ref=send.at[stage, part, k],
            dst_ref=recv.at[stage, part, peer],
            send_sem=send_sem.at[turn, part, k],
            recv_sem=recv_sem.at[turn, part, peer],
            device_id=target[k],
            device_id_type=MESH,
        )

    def start(stage, part, block):
        for k in ORDER:
            send[stage, part, k] = block(slice(k * slots, (k + 1) * slots)).astype(BF16)
        for k in ORDER:
            launch(stage, part, k)

    def launch(stage, part, k):
        @pl.when(live[k])
        def _():
            if stage >= 2:
                copy(stage - 2, part, k, k ^ 1).wait_send()
            copy(stage, part, k, k ^ 1).start()

    def finish(stage, part):
        for k in range(4):

            @pl.when(live[k])
            def _():
                copy(stage, part, k, k).wait_recv()

        return jnp.concatenate([recv[stage, part, k] for k in range(4)], axis=1)

    def build_coupling(first, last):
        step = 16
        base = lax.broadcasted_iota(jnp.int32, (step, LANES), 0)
        for tile in range(own // LANES):
            lanes = slice(tile * LANES, (tile + 1) * LANES)
            columns = [jnp.broadcast_to(columns_ref[j : j + 1, lanes], (step, LANES)) for j in range(entries)]
            values = [jnp.broadcast_to(values_ref[j : j + 1, lanes], (step, LANES)) for j in range(entries)]

            def body(m, carry):
                here = base + m * step
                parts = [jnp.where(columns[j] == here, values[j], 0.0) for j in range(entries)]
                while len(parts) > 1:
                    parts = [sum(parts[i : i + 2][1:], parts[i]) for i in range(0, len(parts), 2)]
                coupling[pl.ds(pl.multiple_of(m * step, step), step), lanes] = parts[0].astype(BF16)
                return carry

            lax.fori_loop(first // step, last // step, body, 0, unroll=4)

    center = 0.5 * (UPPER + LOWER)
    spread = 0.5 * (UPPER - LOWER)
    sigma = center / spread
    half = [x.astype(BF16) for x in residual]
    picked = [dot_nn(x, pick[...]).astype(BF16) for x in half]

    pl.semaphore_wait(barrier, sum(jnp.where(here, 1, 0) for here in live))

    for part in parts:
        start(0, part, lambda lanes: picked[part][:, lanes])

    ratio = 1.0 / sigma
    direction = [None] * PARTS
    solution = [None] * PARTS
    stage = 0
    for iteration in range(ITERS):
        if iteration == 0:
            for load in loads[3:8]:
                load.wait()
            diag = diag_ref[...]
            own_weight = own_ref[...]
            weights = []
            for k in range(4):
                inside = slot_id < jnp.where(live[k], count_ref[0, k], 0)
                weights.append(jnp.where(inside, copy_ref[k : k + 1, :], 0.0))
            weight = jnp.concatenate(weights, axis=1)
            high = weight.astype(BF16)
            rest = weight - high.astype(F32)
            middle = rest.astype(BF16)
            low = (rest - middle.astype(F32)).astype(BF16)
            pieces = jnp.concatenate([jnp.broadcast_to(x, (16, 4 * slots)) for x in (high, middle, low)], axis=0)
            spread_weight = dot_nt(pieces, pick[...])
            denominator = own_weight + (spread_weight[0:1] + spread_weight[16:17] + spread_weight[32:33])
            inverse_denominator = 1.0 / denominator
            build_coupling(0, total // 2)
            loads[8].wait()
        for part in parts:
            ahead[part] = dot_nt(half[part], inverse[own:, :own])
        for part in parts:
            held[part] = dot_nt(half[part], inverse[:own, :own])
        ghosts = [None] * PARTS
        for part in parts:
            ghosts[part] = finish(stage, part)
            whole = ahead[part] + dot_nt(ghosts[part], inverse[own:, own:])
            start(stage + 1, part, lambda lanes: whole[:, lanes])
        for part in parts:
            held[part] = own_weight * (held[part] + dot_nt(ghosts[part], inverse[:own, own:]))
        if iteration == 0:
            build_coupling(total // 2, total)
        else:
            ratio_next = 1.0 / (2.0 * sigma - ratio)
        for part in parts:
            returned = finish(stage + 1, part)
            weighted = (weight * returned.astype(F32)).astype(BF16)
            update = (held[part] + dot_nt(weighted, pick[...])) * inverse_denominator
            if iteration == 0:
                direction[part] = update * (1.0 / center)
            else:
                direction[part] = (ratio_next * ratio) * direction[part] + (2.0 * ratio_next / spread) * update
            half[part] = direction[part].astype(BF16)
            whole = dot_nn(half[part], pick[...])
            start(stage + 2, part, lambda lanes: whole[:, lanes])
        if iteration > 0:
            ratio = ratio_next
        for part in parts:
            solution[part] = direction[part] if iteration == 0 else solution[part] + direction[part]
            held[part] = residual[part] - diag * direction[part] - dot_nn(half[part], coupling[:own, :])
        if iteration == ITERS - 1:
            solution_ref[...] = jnp.transpose(jnp.concatenate(solution, axis=0))
        for part in parts:
            ghosts[part] = finish(stage + 2, part)
            residual[part] = held[part] - dot_nn(ghosts[part], coupling[own:, :])
            if iteration < ITERS - 1:
                half[part] = residual[part].astype(BF16)
                whole = dot_nn(half[part], pick[...])
                start(stage + 3, part, lambda lanes: whole[:, lanes])
            else:
                residual_ref[part * rows : (part + 1) * rows, :] = residual[part]
        stage += 3

    for stage in range(max(rounds - 2, 0), rounds):
        for part in parts:
            for k in range(4):

                @pl.when(live[k])
                def _():
                    copy(stage, part, k, k ^ 1).wait_send()


def write_out(solution_in, residual_in, solution_hbm, residual_hbm, flipped, sems):
    own = residual_in.shape[1]
    copies = [pltpu.make_async_copy(solution_in, solution_hbm, sems.at[0])]
    copies[0].start()
    for i in range(own // LANES):
        lanes = slice(i * LANES, (i + 1) * LANES)
        flipped[lanes, :] = jnp.transpose(residual_in[:, lanes])
        copies.append(pltpu.make_async_copy(flipped.at[lanes], residual_hbm.at[lanes], sems.at[1 + i]))
        copies[-1].start()
    for copy in copies:
        copy.wait()


def per_device(n_x, n_y, right_side, prec_diag, prec_values, prec_columns, inverse, send_list, send_count, own_weight, copy_weight):
    own, width = right_side.shape
    total = inverse.shape[1]
    slots = send_list.shape[2]
    rounds = 3 * ITERS
    vmem = pl.BlockSpec(memory_space=pltpu.VMEM)
    hbm = pl.BlockSpec(memory_space=pltpu.HBM)
    fields = (pltpu.VMEM((own, width), F32), pltpu.VMEM((width, own), F32))
    out = jax.ShapeDtypeStruct((own, width), F32)
    results = pl.pallas_call(
        functools.partial(kernel, n_x, n_y),
        out_shape=fields,
        in_specs=[hbm] * 9,
        out_specs=(vmem, vmem),
        scratch_shapes=[
            pltpu.VMEM(right_side.shape, F32),
            pltpu.VMEM((1, own), F32),
            pltpu.VMEM(prec_values.shape, F32),
            pltpu.VMEM(prec_columns.shape, jnp.int32),
            pltpu.VMEM((4, slots), jnp.int32),
            pltpu.SMEM((1, 4), jnp.int32),
            pltpu.VMEM((1, own), F32),
            pltpu.VMEM((4, slots), F32),
            pltpu.VMEM((total, total), BF16),
            pltpu.VMEM((own, 4 * slots), BF16),
            pltpu.VMEM((total, own), BF16),
            pltpu.VMEM((rounds, PARTS, 4, width // PARTS, slots), BF16),
            pltpu.VMEM((rounds, PARTS, 4, width // PARTS, slots), BF16),
            pltpu.VMEM((PARTS, width // PARTS, 4 * slots), F32),
            pltpu.VMEM((PARTS, width // PARTS, own), F32),
            pltpu.SemaphoreType.DMA((9,)),
            pltpu.SemaphoreType.DMA((2, PARTS, 4)),
            pltpu.SemaphoreType.DMA((2, PARTS, 4)),
        ],
        compiler_params=pltpu.CompilerParams(collective_id=0, has_side_effects=True, vmem_limit_bytes=62 * 2**20 + 2**19),
    )(
        right_side,
        prec_diag.reshape(1, own),
        prec_values,
        prec_columns,
        inverse,
        send_list,
        send_count,
        own_weight.reshape(1, own),
        copy_weight,
    )
    return pl.pallas_call(
        write_out,
        out_shape=(out, out),
        in_specs=[vmem, vmem],
        out_specs=(hbm, hbm),
        scratch_shapes=[pltpu.VMEM((own, width), F32), pltpu.SemaphoreType.DMA((1 + own // LANES,))],
        compiler_params=pltpu.CompilerParams(vmem_limit_bytes=16 * 2**20),
    )(*results)


def solution(mesh):
    return jax.shard_map(
        functools.partial(per_device, mesh.shape["gx"], mesh.shape["gy"]),
        mesh=mesh,
        in_specs=(
            P(("gx", "gy"), None),
            P(("gx", "gy")),
            P(None, ("gx", "gy")),
            P(None, ("gx", "gy")),
            P(("gx", "gy"), None, None),
            P(("gx", "gy"), None, None),
            P(("gx", "gy"), None),
            P(("gx", "gy")),
            P(("gx", "gy"), None, None),
        ),
        out_specs=(P(("gx", "gy"), None), P(("gx", "gy"), None)),
        check_vma=False,
    )
```
